512 devices in a mesh: tile: 128 (over z, y_lo, x, core), comp: 4 (over y_hi).
Axes of the slice: x: 4, y: 8 (y_hi: 4, y_lo: 2; y = y_hi * 2 + y_lo), z: 8, core: 2. Of those that a mesh axis runs over, the one named last changes fastest.
Arguments:
- species_concentration: float32 [48, 88, 512, 128], P('comp', None, 'tile'), may hold values from 0.05 to 2
- courant_face_numbers: float32 [2, 88, 512, 128], P(None, 'comp', 'tile'), may hold values from -0.24 to 0.24
- diffusive_interface_factor: float32 [88, 512, 128], P('comp', 'tile'), may hold values from 0.05 to 3
- thermal_anomaly_field: float32 [88, 512, 128], P('comp', 'tile'), may hold values from -6 to 6
- seawater_indicator: int32 [512, 128], P('tile'), may hold values 0 or 1
- wet_layer_number: int32 [512, 128], P('tile'), may hold values from 1 to 88
- species_coupling_matrix: float32 [48, 48], replicated, may hold values from -0.875 to 0.875
- species_photic_factor: float32 [48], replicated, may hold values from -2 to 2
- species_loss_factor: float32 [48], replicated, may hold values from 0.2 to 2
Outputs:
- updated_species_field: float32 [48, 88, 512, 128], P('comp', None, 'tile')
- temperature_out: float32 [88, 512, 128], P('comp', 'tile')
The draws below stay inside these ranges and needn't reach their ends.
All inputs are finite; a program needn't handle non-finite values. No bound on the sum of `seawater_indicator` on one device may be relied on, other than what follows from the above.
Results may differ from the reference program's by a relative error of at most 0.0001.
Values sent between devices are 32-bit elements; how exact they have to be, the bound alone decides.
No kernel may reach another device: no remote copies, remote signals or barrier semaphores. Data moves between devices by JAX's collectives and lax.ppermute only.
A program may use at most 64 MiB of HBM per device.

```python
import math
import jax
import jax.numpy as jnp
from jax import lax

GRID_WIDTH_NORTH = 128
DEPTH_LAYERS = 88
NTR = 48
ADVECT = 2
SUBSTEPS = 4
GRID_WIDTH_EAST = 512


def touch_ends(entries, rng, smallest, top_value):
    longest = entries.shape.index(max(entries.shape))
    spots = []
    for shift in (0, 1):
        where = [jax.random.randint(jax.random.fold_in(rng, axis), (), 0, length) for axis, length in enumerate(entries.shape)]
        where[longest] = (where[longest] + shift) % entries.shape[longest]
        spots.append(tuple(where))
    return entries.at[spots[0]].set(smallest).at[spots[1]].set(top_value)


def block_levels(own_key, dims, pieces, low, largest):
    def one(axis_at, parts):
        heights = jax.random.uniform(jax.random.fold_in(jax.random.fold_in(own_key, 6), axis_at), (parts,), jnp.float32, low / len(pieces), largest / len(pieces))
        return jnp.repeat(jnp.exp(heights), dims[axis_at] // parts).reshape((-1,) + (1,) * (len(dims) - axis_at - 1))

    factor_of = one(*pieces[0])
    for cut in pieces[1:]:
        factor_of = factor_of * one(*cut)
    return factor_of


def noise(stream_key, extent, deviation, limit, shards=(), held_as=jnp.bfloat16):
    entries = deviation * jax.random.normal(stream_key, extent, jnp.float32)
    if shards:
        entries = entries * block_levels(stream_key, extent, shards, -0.22, 0.18)
    return jnp.clip(entries, -limit, limit).astype(held_as)


def setup_inputs(seed: int = 0) -> dict:
    splits = jax.random.split(jax.random.key(seed), 10)
    return {
        "species_concentration": jnp.clip(jnp.exp(math.log(2.0) - 3.6888794 * jax.random.uniform(splits[0], (NTR, DEPTH_LAYERS, GRID_WIDTH_EAST, GRID_WIDTH_NORTH), jnp.float32) ** block_levels(splits[0], (NTR, DEPTH_LAYERS, GRID_WIDTH_EAST, GRID_WIDTH_NORTH), ((0, 4), (2, 128)), -0.2, 0.2)), 0.05, 2.0),
        "courant_face_numbers": jnp.clip(jax.random.uniform(splits[1], (2, DEPTH_LAYERS, GRID_WIDTH_EAST, GRID_WIDTH_NORTH), jnp.float32, -0.24, 0.24) * block_levels(splits[1], (2, DEPTH_LAYERS, GRID_WIDTH_EAST, GRID_WIDTH_NORTH), ((1, 4), (2, 128)), -0.4, 0.0), -0.24, 0.24),
        "diffusive_interface_factor": jnp.clip(jnp.exp(math.log(3.0) - 4.0943445 * jax.random.uniform(splits[2], (DEPTH_LAYERS, GRID_WIDTH_EAST, GRID_WIDTH_NORTH), jnp.float32) ** block_levels(splits[2], (DEPTH_LAYERS, GRID_WIDTH_EAST, GRID_WIDTH_NORTH), ((0, 4), (1, 128)), -0.2, 0.2)), 0.05, 3.0),
        "thermal_anomaly_field": noise(splits[3], (DEPTH_LAYERS, GRID_WIDTH_EAST, GRID_WIDTH_NORTH), 1.0, 6.0, ((0, 4), (1, 128)), jnp.float32),
        "seawater_indicator": touch_ends((jax.random.randint(splits[4], (GRID_WIDTH_EAST, GRID_WIDTH_NORTH), 0, 5) < 4).astype(jnp.int32), jax.random.fold_in(splits[4], 1), 0, 1),
        "wet_layer_number": touch_ends(jax.random.randint(splits[5], (GRID_WIDTH_EAST, GRID_WIDTH_NORTH), 1, DEPTH_LAYERS + 1), jax.random.fold_in(splits[5], 1), 1, DEPTH_LAYERS).astype(jnp.int32),
        "species_coupling_matrix": noise(splits[6], (NTR, NTR), NTR ** -0.5, 0.875, (), jnp.float32),
        "species_photic_factor": jnp.clip(jax.random.uniform(splits[7], (NTR,), jnp.float32, -2.0, 2.0), -2.0, 2.0),
        "species_loss_factor": jnp.clip(jnp.exp(jax.random.uniform(splits[8], (NTR,), jnp.float32, math.log(0.2), math.log(2.0))), 0.2, 2.0),
    }


RATE_STEP = 0.25
HEAT_GAIN = 2.0


def activity(seawater_indicator, wet_layer_number, first_level, count):
    level_index = first_level + jnp.arange(count, dtype=jnp.int32)
    inside = (level_index[:, None, None] < wet_layer_number[None]) & (seawater_indicator[None] > 0)
    return inside.astype(jnp.float32)


def advance(conc, active, east, north):
    open_east = active[:, :-1] * active[:, 1:]
    speed_east = east[:, :-1] * open_east
    flux_east = jnp.maximum(speed_east, 0.0) * conc[:, :, :-1] + jnp.minimum(speed_east, 0.0) * conc[:, :, 1:]
    inner = conc[:, :, 1:-1]
    active_inner = active[:, 1:-1]
    open_north = active_inner[:, :, :-1] * active_inner[:, :, 1:]
    speed_north = north[:, 1:-1, :-1] * open_north
    flux_north = jnp.maximum(speed_north, 0.0) * inner[..., :-1] + jnp.minimum(speed_north, 0.0) * inner[..., 1:]
    flux_north = jnp.pad(flux_north, ((0, 0), (0, 0), (0, 0), (1, 1)))
    return inner - (flux_east[:, :, 1:] - flux_east[:, :, :-1]) - (flux_north[..., 1:] - flux_north[..., :-1])


def diffuse(conc, diffusive_interface_factor, active):
    levels = conc.shape[1]
    coupling = diffusive_interface_factor[:-1] * active[:-1] * active[1:]
    nothing = jnp.zeros_like(diffusive_interface_factor[0])
    ratios = []
    partial_list = []
    for level in range(levels):
        coupling_up = coupling[level - 1] if level > 0 else nothing
        coupling_down = coupling[level] if level < levels - 1 else nothing
        pivot = 1.0 + coupling_up + coupling_down
        source = conc[:, level]
        if level > 0:
            pivot = pivot + coupling_up * ratios[-1]
            source = source + coupling_up * partial_list[-1]
        ratios.append(-coupling_down / pivot)
        partial_list.append(source / pivot)
    solved = [partial_list[-1]]
    for level in range(levels - 2, -1, -1):
        solved.append(partial_list[level] - ratios[level] * solved[-1])
    solved = solved[::-1]
    return jnp.stack(solved, axis=1)


def reaction(conc, light_level, active, species_coupling_matrix, species_photic_factor, species_loss_factor):
    layout_shape = conc.shape
    columns_flat = conc.reshape(layout_shape[0], -1)
    light_flat = light_level.reshape(1, -1)
    active_flat = active.reshape(1, -1)
    for substep in range(SUBSTEPS):
        forcing = jnp.dot(species_coupling_matrix, columns_flat, precision=lax.Precision.HIGHEST, preferred_element_type=jnp.float32)
        forcing = forcing + species_photic_factor[:, None] * light_flat
        columns_flat = columns_flat + RATE_STEP * active_flat * (jnp.tanh(forcing) - species_loss_factor[:, None] * columns_flat)
    return columns_flat.reshape(layout_shape)


def reference(species_concentration, courant_face_numbers, diffusive_interface_factor, thermal_anomaly_field, seawater_indicator, wet_layer_number, species_coupling_matrix, species_photic_factor, species_loss_factor):
    active = activity(seawater_indicator, wet_layer_number, 0, DEPTH_LAYERS)
    padding = ((0, 0), (1, 1), (0, 0))
    active_pad = jnp.pad(active, padding)
    east_pad = jnp.pad(courant_face_numbers[0], padding)
    north_pad = jnp.pad(courant_face_numbers[1], padding)

    def transport(single):
        current = single[None]
        for advect_step in range(ADVECT):
            current = advance(jnp.pad(current, ((0, 0), (0, 0), (1, 1), (0, 0))), active_pad, east_pad, north_pad)
        return diffuse(current, diffusive_interface_factor, active)[0]

    advected = lax.map(transport, species_concentration)
    attenuation = 0.05 + 0.1 * advected[0]
    optical_depth = jnp.cumsum(attenuation, axis=0) - attenuation
    light_level = jnp.exp(-optical_depth)

    def per_level(level_items):
        return reaction(level_items[0], level_items[1], level_items[2], species_coupling_matrix, species_photic_factor, species_loss_factor)

    reacted = lax.map(per_level, (jnp.moveaxis(advected, 1, 0), light_level, active))
    updated_species_field = jnp.moveaxis(reacted, 0, 1)
    sunlight_warming = HEAT_GAIN * active * light_level * (1.0 - jnp.exp(-attenuation))
    return updated_species_field, thermal_anomaly_field + sunlight_warming
```

```python
import jax
import jax.numpy as jnp
from jax import lax
from jax.experimental import pallas as pl
from jax.experimental.pallas import tpu as pltpu
from jax.sharding import PartitionSpec as P

ADVECT = 2
SUBSTEPS = 4
RATE_STEP = 0.25
HEAT_GAIN = 2.0
LANES = 128
HALO = 2
ROWS = 8
F32 = jnp.float32
BF16 = jnp.bfloat16
VMEM = pl.BlockSpec(memory_space=pltpu.VMEM)
SMEM = pl.BlockSpec(memory_space=pltpu.SMEM)


def call(kernel, outs, scratch=(), ins=None, mib=24):
    return pl.pallas_call(
        kernel,
        out_shape=outs,
        in_specs=ins,
        out_specs=jax.tree.map(lambda _: VMEM, outs),
        scratch_shapes=list(scratch),
        compiler_params=pltpu.CompilerParams(vmem_limit_bytes=mib << 20),
    )


def iota(shape, dim):
    return lax.broadcasted_iota(jnp.int32, shape, dim)


def split3(x):
    hi = x.astype(BF16)
    rest = x - hi.astype(F32)
    mid = rest.astype(BF16)
    low = (rest - mid.astype(F32)).astype(BF16)
    return hi, mid, low


def picked(x, onehot):
    total = None
    for part in split3(x):
        term = jnp.dot(part, onehot, preferred_element_type=F32)
        total = term if total is None else total + term
    return total


def pairing_kernel(levels, depth_ref, fold_ref, unfold_ref, rank_ref, lane_ref):
    width = depth_ref.shape[0]
    columns = width * LANES
    lanes = columns // 2
    depth = depth_ref[...]
    wide = jnp.concatenate([depth] * (LANES // width), axis=0)
    upright = wide.T
    a = jnp.zeros((1, lanes), F32)
    b = jnp.zeros((1, lanes), F32)
    rank_ref[...] = jnp.zeros_like(rank_ref)
    for i in range(width):
        own_col = upright[:, i : i + 1]
        own_row = depth[i : i + 1, :]
        rank_col = jnp.zeros((LANES, 1), F32)
        rank_row = jnp.zeros((1, LANES), F32)
        mine_col = i * LANES + iota((LANES, LANES), 0)
        mine_row = i * LANES + iota((LANES, LANES), 1)
        for o in range(width):
            other_row = depth[o : o + 1, :]
            other_col = upright[:, o : o + 1]
            index_row = o * LANES + iota((LANES, LANES), 1)
            index_col = o * LANES + iota((LANES, LANES), 0)
            ahead = (other_row > own_col) | ((other_row == own_col) & (index_row < mine_col))
            rank_col = rank_col + jnp.sum(jnp.where(ahead, 1.0, 0.0), axis=1, keepdims=True)
            ahead = (other_col > own_row) | ((other_col == own_row) & (index_col < mine_row))
            rank_row = rank_row + jnp.sum(jnp.where(ahead, 1.0, 0.0), axis=0, keepdims=True)
        half = float(lanes)
        last = float(columns - 1)
        lane_col = jnp.where(rank_col < half, rank_col, last - rank_col)
        hit = lane_col == iota((LANES, lanes), 1).astype(F32)
        fold_ref[i] = jnp.where(hit, 1.0, 0.0).astype(BF16)
        deep = hit & (rank_col < half)
        a = a + jnp.sum(jnp.where(deep, own_col, 0.0), axis=0, keepdims=True)
        b = b + jnp.sum(jnp.where(hit & (rank_col >= half), own_col, 0.0), axis=0, keepdims=True)
        lane_row = jnp.where(rank_row < half, rank_row, last - rank_row)
        unfold_ref[:, i * LANES : (i + 1) * LANES] = jnp.where(
            lane_row == iota((lanes, LANES), 0).astype(F32), 1.0, 0.0
        ).astype(BF16)
        rank_ref[i : i + 1, :] = rank_row
    lane_ref[...] = jnp.zeros_like(lane_ref)
    lane_ref[0:1, :] = a
    lane_ref[1:2, :] = b
    over = jnp.max(jnp.where(a + b > float(levels), 1.0, 0.0), axis=1, keepdims=True)
    lane_ref[2:3, :] = jnp.broadcast_to(over, (1, lanes))


def pack(deep, shallow, x_ref, fold_ref, out_ref, depth, levels, groups):
    pass


def transport_kernel(
    c_ref, face_ref, depth_ref, side_ref, fold_ref, out_ref, x_ref, ratio_ref
):
    groups, levels = c_ref.shape[:2]
    half = levels // 2
    depth = depth_ref[...]
    row = iota((ROWS, LANES), 0)
    lane = iota((ROWS, LANES), 1)
    inner_east = row < ROWS - 1
    inner_north = lane < LANES - 1
    zero = jnp.zeros((ROWS, LANES), F32)
    one = jnp.ones((ROWS, LANES), F32)

    def active_at(k):
        return jnp.where(depth > k.astype(F32), 1.0, 0.0)

    def forward(k, carry):
        active, gone, ratio, *before = carry
        below = active_at(k + 1)
        u, v, mix = face_ref[0, k], face_ref[1, k], face_ref[2, k]
        u = jnp.where(inner_east, u * active * pltpu.roll(active, ROWS - 1, 0), 0.0)
        v = jnp.where(inner_north, v * active * pltpu.roll(active, LANES - 1, 1), 0.0)
        up, um = jnp.maximum(u, 0.0), jnp.minimum(u, 0.0)
        vp, vm = jnp.maximum(v, 0.0), jnp.minimum(v, 0.0)
        west, south = pltpu.roll(up, 1, 0), pltpu.roll(vp, 1, 1)
        own = (one - up + pltpu.roll(um, 1, 0)) + (pltpu.roll(vm, 1, 1) - vp)
        down = jnp.where(k < levels - 1, mix * active * below, 0.0)
        inverse = 1.0 / (1.0 + gone + down + gone * ratio)
        new_ratio = -down * inverse
        ratio_ref[k] = new_ratio
        after = []
        for t in range(groups):
            c = c_ref[t, k]
            for _ in range(ADVECT):
                c = (
                    own * c
                    + west * pltpu.roll(c, 1, 0)
                    - um * pltpu.roll(c, ROWS - 1, 0)
                    + south * pltpu.roll(c, 1, 1)
                    - vm * pltpu.roll(c, LANES - 1, 1)
                )
            p = (c + gone * before[t]) * inverse
            x_ref[pl.ds(pl.multiple_of((k * groups + t) * ROWS, ROWS), ROWS), :] = p
            after.append(p)
        return (below, down, new_ratio, *after)

    start = (active_at(jnp.int32(0)), zero, zero, *([zero] * groups))
    lax.fori_loop(0, levels, forward, start)

    def at(k, t):
        return pl.ds(pl.multiple_of((k * groups + t) * ROWS, ROWS), ROWS)

    def back_low(n, x):
        k = levels - 1 - n
        ratio = ratio_ref[k]
        new = []
        for t in range(groups):
            value = x_ref[at(k, t), :] - ratio * x[t]
            x_ref[at(k, t), :] = value
            new.append(value)
        return tuple(new)

    side = side_ref[...]
    deep_depth = jnp.where(side > 0.5, depth, 0.0)
    shallow_depth = jnp.where(side < -0.5, depth, 0.0)

    def back_high(n, x):
        k = half - 1 - n
        other = levels - 1 - k
        ratio = ratio_ref[k]
        low, high = k.astype(F32), other.astype(F32)
        deep_low, deep_high = deep_depth > low, deep_depth > high
        shallow_low, shallow_high = shallow_depth > low, shallow_depth > high
        new = []
        for t in range(groups):
            value = x_ref[at(k, t), :] - ratio * x[t]
            under = x_ref[at(other, t), :]
            new.append(value)
            x_ref[at(k, t), :] = jnp.where(deep_low, value, jnp.where(shallow_high, under, 0.0))
            x_ref[at(other, t), :] = jnp.where(deep_high, under, jnp.where(shallow_low, value, 0.0))
        return tuple(new)

    x = lax.fori_loop(0, half, back_low, tuple([zero] * groups))
    lax.fori_loop(0, half, back_high, x)

    width = fold_ref.shape[0]
    step = 4
    rows = step * groups
    left = iota((rows, LANES), 1) < LANES // 2

    def folded(k):
        parts = []
        for i in range(width):
            first = pl.multiple_of(k * groups * ROWS, ROWS) + HALO + i
            parts.append(x_ref[pl.ds(first, rows, stride=ROWS), :])
        whole = jnp.concatenate(parts, axis=1)
        onehot = jnp.concatenate([fold_ref[i] for i in range(width)], axis=0)
        return picked(whole, onehot)

    def send(n, _):
        k = n * step
        upper, lower = folded(k), folded(k + half)
        here = pl.ds(pl.multiple_of(k * groups, rows), rows)
        for v in range(upper.shape[1] // LANES):
            u = upper[:, v * LANES : (v + 1) * LANES]
            w = lower[:, v * LANES : (v + 1) * LANES]
            out_ref[2 * v, here, :] = jnp.where(left, u, pltpu.roll(w, LANES // 2, 1))
            out_ref[2 * v + 1, here, :] = jnp.where(left, pltpu.roll(u, LANES // 2, 1), w)
        return 0

    lax.fori_loop(0, half // step, send, 0)


def reaction_kernel(
    x_ref, lane_ref, matrix_ref, decay_ref, photic_ref, out_ref, state_ref, light_ref, chl_ref
):
    peers, rows, _ = x_ref.shape
    groups = matrix_ref.shape[0] // (2 * peers)
    half = rows // groups
    quarter = half // 2
    pad = light_ref.shape[0]
    chl_ref[...] = jnp.zeros_like(chl_ref)
    for k in range(half):
        chl_ref[k : k + 1, :] = x_ref[0, k * groups : k * groups + 1, :]
    attenuation = jnp.where(iota((pad, LANES), 0) < half, 0.05 + 0.1 * chl_ref[...], 0.0)
    before = jnp.where(iota((pad, pad), 1) < iota((pad, pad), 0), 1.0, 0.0).astype(F32)
    beyond = jnp.where(iota((pad, pad), 1) > iota((pad, pad), 0), 1.0, 0.0).astype(F32)
    above = jnp.dot(before, attenuation, precision=lax.Precision.HIGHEST, preferred_element_type=F32)
    under = jnp.dot(beyond, attenuation, precision=lax.Precision.HIGHEST, preferred_element_type=F32)
    total = jnp.broadcast_to(jnp.sum(attenuation, axis=0, keepdims=True), (pad, LANES))
    total = pltpu.roll(total, LANES // 2, 1)
    right = iota((pad, LANES), 1) >= LANES // 2
    above = above + jnp.where(right, total, 0.0)
    under = under + jnp.where(right, 0.0, total)
    level = (iota((pad, LANES), 0) + jnp.where(right, half, 0)).astype(F32)
    deep = level < lane_ref[0:1, :]
    light = jnp.exp(-jnp.where(deep, above, under))
    light_ref[...] = light
    heat = HEAT_GAIN * light * (1.0 - jnp.exp(-attenuation))
    chl_ref[...] = heat
    first, second = chl_ref[0:quarter, :], chl_ref[quarter : 2 * quarter, :]
    left = iota((quarter, LANES), 1) < LANES // 2
    outer, inner = jnp.where(left, first, second), jnp.where(left, second, first)
    for q in range(peers):
        out_ref[q, rows:, :] = jnp.zeros((out_ref.shape[1] - rows, LANES), F32)
        out_ref[q, rows : rows + quarter, :] = outer if q in (0, peers - 1) else inner

    span = 2 * groups
    decay = decay_ref[...]
    matrix = matrix_ref[...]
    hi = matrix.astype(BF16)
    low = (matrix - hi.astype(F32)).astype(BF16)
    both = jnp.concatenate([hi, hi], axis=1)
    photic_even, photic_odd = photic_ref[0], photic_ref[1]

    def run(pairs):
        state, push = [], []
        for m in pairs:
            state.append(
                jnp.concatenate([x_ref[s, m * span : (m + 1) * span, :] for s in range(peers)], axis=0)
            )
            push.append(
                photic_even * light_ref[2 * m : 2 * m + 1, :]
                + photic_odd * light_ref[2 * m + 1 : 2 * m + 2, :]
            )
        state, push = jnp.concatenate(state, axis=1), jnp.concatenate(push, axis=1)
        rate = jnp.concatenate([decay] * len(pairs), axis=1)
        for _ in range(SUBSTEPS):
            upper = state.astype(BF16)
            lower = (state - upper.astype(F32)).astype(BF16)
            forcing = (
                jnp.dot(both, jnp.concatenate([upper, lower], axis=0), preferred_element_type=F32)
                + jnp.dot(low, upper, preferred_element_type=F32)
                + push
            )
            state = state * rate + RATE_STEP * jnp.tanh(forcing)
        for n, m in enumerate(pairs):
            for s in range(peers):
                out_ref[s, m * span : (m + 1) * span, :] = state[
                    s * span : (s + 1) * span, n * LANES : (n + 1) * LANES
                ]

    for m in range(0, half // 2, 2):
        run((m, m + 1))


def return_kernel(
    x_ref, c_ref, thermal_ref, depth_ref, side_ref, unfold_ref, place_ref, out_ref, heat_ref, y_ref, h_ref
):
    groups, levels, width, _ = c_ref.shape
    share = thermal_ref.shape[0]
    half = levels // 2
    step = 4
    rows = step * groups
    left = iota((rows, LANES), 1) < LANES // 2
    unfold = unfold_ref[...]

    def spread(k, value):
        whole = picked(value, unfold)
        for i in range(width):
            first = pl.multiple_of(k * groups * ROWS, ROWS) + i
            y_ref[pl.ds(first, rows, stride=ROWS), :] = whole[:, i * LANES : (i + 1) * LANES]

    def open_up(n, _):
        k = n * step
        here = pl.ds(pl.multiple_of(k * groups, rows), rows)
        upper, lower = [], []
        for v in range(x_ref.shape[0] // 2):
            p, q = x_ref[2 * v, here, :], x_ref[2 * v + 1, here, :]
            upper.append(jnp.where(left, p, pltpu.roll(q, LANES // 2, 1)))
            lower.append(jnp.where(left, pltpu.roll(p, LANES // 2, 1), q))
        spread(k, jnp.concatenate(upper, axis=1))
        spread(k + half, jnp.concatenate(lower, axis=1))
        return 0

    lax.fori_loop(0, half // step, open_up, 0)

    depth = depth_ref[...]
    side = side_ref[...]
    deep_depth = jnp.where(side > 0.5, depth, 0.0)
    shallow_depth = jnp.where(side < -0.5, depth, 0.0)

    def merge(k, _):
        other = levels - 1 - k
        deep = deep_depth > k.astype(F32)
        shallow = shallow_depth > k.astype(F32)
        for t in range(groups):
            one = y_ref[pl.ds(pl.multiple_of((k * groups + t) * ROWS, ROWS), width), :]
            two = y_ref[pl.ds(pl.multiple_of((other * groups + t) * ROWS, ROWS), width), :]
            out_ref[t, k] = jnp.where(deep, one, jnp.where(shallow, two, c_ref[t, k]))
        return 0

    lax.fori_loop(0, levels, merge, 0)

    place = place_ref[0]
    begin = groups * half
    halves = ([], [])
    left = iota((share, LANES), 1) < LANES // 2
    for v in range(x_ref.shape[0] // 2):
        p, q = (x_ref[2 * v + n, begin : begin + share, :] for n in (0, 1))
        halves[0].append(jnp.where(left, p, pltpu.roll(q, LANES // 2, 1)))
        halves[1].append(jnp.where(left, pltpu.roll(p, LANES // 2, 1), q))
    first, second = (jnp.concatenate(h, axis=1) for h in halves)
    upper_half = place < 2
    deep_heat = jnp.where(upper_half, first, second)
    shallow_heat = jnp.where(upper_half, second, first)
    flip = jnp.where(iota((share, share), 0) + iota((share, share), 1) == share - 1, 1.0, 0.0)
    shallow_heat = jnp.dot(
        flip.astype(F32), shallow_heat, precision=lax.Precision.HIGHEST, preferred_element_type=F32
    )
    for n, part in enumerate((deep_heat, shallow_heat)):
        whole = picked(part, unfold)
        for i in range(width):
            h_ref[n, pl.ds(i, share, stride=ROWS), :] = whole[:, i * LANES : (i + 1) * LANES]
    for k in range(share):
        level = (place * share + k).astype(F32)
        one, two = h_ref[0, k * ROWS : k * ROWS + width, :], h_ref[1, k * ROWS : k * ROWS + width, :]
        warm = jnp.where(deep_depth > level, one, jnp.where(shallow_depth > level, two, 0.0))
        heat_ref[k] = thermal_ref[k] + warm


def ring(axis):
    count = lax.axis_size(axis)
    forward = [(i, i + 1) for i in range(count - 1)]
    return forward, [(b, a) for a, b in forward]


def edges(block, dim):
    forward, backward = ring("tile")
    size = block.shape[dim]
    low = lax.ppermute(lax.slice_in_dim(block, size - HALO, size, axis=dim), "tile", forward)
    high = lax.ppermute(lax.slice_in_dim(block, 0, HALO, axis=dim), "tile", backward)
    return low, high


def body(
    species_concentration,
    courant_face_numbers,
    diffusive_interface_factor,
    thermal_anomaly_field,
    seawater_indicator,
    wet_layer_number,
    species_coupling_matrix,
    species_photic_factor,
    species_loss_factor,
):
    groups, levels, width, _ = species_concentration.shape
    share = diffusive_interface_factor.shape[0]
    peers = lax.axis_size("comp")
    half = levels // 2
    columns = width * LANES
    lanes = columns // 2
    place = lax.axis_index("comp")
    sds = jax.ShapeDtypeStruct

    depth = jnp.where(seawater_indicator > 0, wet_layer_number, 0).astype(F32)
    flat = jnp.concatenate(
        [species_concentration.reshape(groups * levels, width, LANES), depth[None]], axis=0
    )
    c_low, c_high = edges(flat, 1)
    slices = jnp.concatenate([courant_face_numbers, diffusive_interface_factor[None]], axis=0)
    faces = lax.all_gather(slices, "comp", axis=1, tiled=True)
    f_low, f_high = edges(faces[:2], 2)

    fold, unfold, rank, lane_depth = call(
        lambda *refs: pairing_kernel(levels, *refs),
        (
            sds((width, LANES, lanes), BF16),
            sds((lanes, columns), BF16),
            sds((ROWS, LANES), F32),
            sds((ROWS, lanes), F32),
        ),
        ins=[VMEM],
    )(depth)
    rank = rank[:width]
    over = lane_depth[2, 0] > 0.5
    deep = rank < float(lanes)
    split = groups * levels
    own_ext = jnp.concatenate(
        [c_low[:split], species_concentration.reshape(split, width, LANES), c_high[:split]], axis=1
    ).reshape(groups, levels, ROWS, LANES)
    depth_ext = jnp.concatenate([c_low[split], depth, c_high[split]], axis=0)
    gap = jnp.zeros((1, levels, HALO, LANES), F32)
    face_ext = jnp.concatenate(
        [
            jnp.concatenate([f_low, gap], axis=0),
            faces,
            jnp.concatenate([f_high, gap], axis=0),
        ],
        axis=2,
    )

    eye = jnp.eye(2, dtype=F32)
    matrix = species_coupling_matrix.reshape(peers, groups, peers, groups)
    matrix = matrix[:, None, :, :, None, :] * eye[None, :, None, None, :, None]
    matrix = matrix.reshape(peers * 2 * groups, peers * 2 * groups)

    def spreadable(vector):
        v = jnp.broadcast_to(vector.reshape(peers, 1, groups, 1), (peers, 2, groups, LANES))
        return v

    decay = spreadable(1.0 - RATE_STEP * species_loss_factor).reshape(-1, LANES)
    photic = spreadable(species_photic_factor)[None] * eye[:, None, :, None, None]
    photic = photic.reshape(2, -1, LANES)

    def round_trip(current, temperature, side, a, b):
        side_ext = jnp.pad(side, ((HALO, HALO), (0, 0)))
        folded = call(
            transport_kernel,
            sds((peers, half * groups, LANES), F32),
            scratch=[
                pltpu.VMEM((levels * groups * ROWS, LANES), F32),
                pltpu.VMEM((levels, ROWS, LANES), F32),
            ],
            ins=[VMEM] * 5,
        )(own_ext, face_ext, depth_ext, side_ext, fold)
        arrived = lax.all_to_all(folded, "comp", split_axis=0, concat_axis=0, tiled=True)
        part = lanes // peers
        mine = lax.dynamic_slice_in_dim(jnp.stack([a, b]), place * part, part, axis=1)
        mine = jnp.pad(jnp.concatenate([mine, mine], axis=1), ((0, ROWS - 2), (0, 0)))
        extra = -(-share // ROWS) * ROWS
        reacted = call(
            reaction_kernel,
            sds((peers, half * groups + extra, LANES), F32),
            scratch=[
                pltpu.VMEM((ROWS, LANES), F32),
                pltpu.VMEM((-(-half // ROWS) * ROWS, LANES), F32),
                pltpu.VMEM((-(-half // ROWS) * ROWS, LANES), F32),
            ],
            ins=[VMEM] * 5,
        )(arrived, mine, matrix, decay, photic)
        returned = lax.all_to_all(reacted, "comp", split_axis=0, concat_axis=0, tiled=True)
        return call(
            return_kernel,
            (
                sds((groups, levels, width, LANES), F32),
                sds((share, width, LANES), F32),
            ),
            scratch=[
                pltpu.VMEM((levels * groups * ROWS, LANES), F32),
                pltpu.VMEM((2, -(-share // ROWS) * ROWS * ROWS, LANES), F32),
            ],
            ins=[VMEM] * 6 + [SMEM],
        )(returned, current, temperature, depth, side, unfold, place[None].astype(jnp.int32))

    a, b = lane_depth[0], lane_depth[1]
    sign = jnp.where(deep, 1.0, -1.0).astype(F32)
    side = jnp.where(over & ~deep, 0.0, sign)
    out, heat = round_trip(
        species_concentration, thermal_anomaly_field, side, a, jnp.where(over, 0.0, b)
    )

    def rest(carry):
        _, current, temperature = carry
        current, temperature = round_trip(
            current, temperature, jnp.where(deep, 0.0, sign), jnp.zeros_like(a), b
        )
        return jnp.zeros((), bool), current, temperature

    _, out, heat = lax.while_loop(lambda carry: carry[0], rest, (over, out, heat))
    return out, heat


def solution(mesh):
    in_specs = (
        P("comp", None, "tile", None),
        P(None, "comp", "tile", None),
        P("comp", "tile", None),
        P("comp", "tile", None),
        P("tile", None),
        P("tile", None),
        P(),
        P(),
        P(),
    )
    out_specs = (P("comp", None, "tile", None), P("comp", "tile", None))
    return jax.shard_map(body, mesh=mesh, in_specs=in_specs, out_specs=out_specs, check_vma=False)
```

```python
import jax
import jax.numpy as jnp
from jax import lax
from jax.experimental import pallas as pl
from jax.experimental.pallas import tpu as pltpu
from jax.sharding import PartitionSpec as P

ADVECT = 2
SUBSTEPS = 4
RATE_STEP = 0.25
HEAT_GAIN = 2.0
LANES = 128
HALO = 2
ROWS = 8
PAD = 16
F32 = jnp.float32
BF16 = jnp.bfloat16
VMEM = pl.BlockSpec(memory_space=pltpu.VMEM)
SMEM = pl.BlockSpec(memory_space=pltpu.SMEM)


def call(kernel, outs, scratch=(), ins=None, mib=24):
    return pl.pallas_call(
        kernel,
        out_shape=outs,
        in_specs=ins,
        out_specs=jax.tree.map(lambda _: VMEM, outs),
        scratch_shapes=list(scratch),
        compiler_params=pltpu.CompilerParams(vmem_limit_bytes=mib << 20),
    )


def iota(shape, dim):
    return lax.broadcasted_iota(jnp.int32, shape, dim)


def split3(x):
    hi = x.astype(BF16)
    rest = x - hi.astype(F32)
    mid = rest.astype(BF16)
    low = (rest - mid.astype(F32)).astype(BF16)
    return hi, mid, low


def picked(x, onehot):
    size = x.shape[0]
    full = -(-size // PAD) * PAD
    if full != size:
        x = jnp.concatenate([x, jnp.zeros((full - size, x.shape[1]), F32)], axis=0)
    stack = jnp.concatenate(split3(x), axis=0)
    whole = jnp.dot(stack, onehot, preferred_element_type=F32)
    return (whole[:size] + whole[full : full + size]) + whole[2 * full : 2 * full + size]


def pairing_kernel(levels, depth_ref, fold_ref, unfold_ref, rank_ref, lane_ref):
    width = depth_ref.shape[0]
    columns = width * LANES
    lanes = columns // 2
    depth = depth_ref[...]
    wide = jnp.concatenate([depth] * (LANES // width), axis=0)
    upright = wide.T
    a = jnp.zeros((1, lanes), F32)
    b = jnp.zeros((1, lanes), F32)
    rank_ref[...] = jnp.zeros_like(rank_ref)
    for i in range(width):
        own_col = upright[:, i : i + 1]
        own_row = depth[i : i + 1, :]
        rank_col = jnp.zeros((LANES, 1), F32)
        rank_row = jnp.zeros((1, LANES), F32)
        mine_col = i * LANES + iota((LANES, LANES), 0)
        mine_row = i * LANES + iota((LANES, LANES), 1)
        for o in range(width):
            other_row = depth[o : o + 1, :]
            other_col = upright[:, o : o + 1]
            index_row = o * LANES + iota((LANES, LANES), 1)
            index_col = o * LANES + iota((LANES, LANES), 0)
            ahead = (other_row > own_col) | ((other_row == own_col) & (index_row < mine_col))
            rank_col = rank_col + jnp.sum(jnp.where(ahead, 1.0, 0.0), axis=1, keepdims=True)
            ahead = (other_col > own_row) | ((other_col == own_row) & (index_col < mine_row))
            rank_row = rank_row + jnp.sum(jnp.where(ahead, 1.0, 0.0), axis=0, keepdims=True)
        half = float(lanes)
        last = float(columns - 1)
        lane_col = jnp.where(rank_col < half, rank_col, last - rank_col)
        hit = lane_col == iota((LANES, lanes), 1).astype(F32)
        fold_ref[i] = jnp.where(hit, 1.0, 0.0).astype(BF16)
        deep = hit & (rank_col < half)
        a = a + jnp.sum(jnp.where(deep, own_col, 0.0), axis=0, keepdims=True)
        b = b + jnp.sum(jnp.where(hit & (rank_col >= half), own_col, 0.0), axis=0, keepdims=True)
        lane_row = jnp.where(rank_row < half, rank_row, last - rank_row)
        unfold_ref[:, i * LANES : (i + 1) * LANES] = jnp.where(
            lane_row == iota((lanes, LANES), 0).astype(F32), 1.0, 0.0
        ).astype(BF16)
        rank_ref[i : i + 1, :] = rank_row
    lane_ref[...] = jnp.zeros_like(lane_ref)
    lane_ref[0:1, :] = a
    lane_ref[1:2, :] = b
    over = jnp.max(jnp.where(a + b > float(levels), 1.0, 0.0), axis=1, keepdims=True)
    lane_ref[2:3, :] = jnp.broadcast_to(over, (1, lanes))


def split_kernel(c_ref, face_ref, sea_ref, wet_ref, west_a, west_b, east_a, east_b, depth_ref):
    width = sea_ref.shape[0]
    half = west_a.shape[1] // PAD
    levels = 2 * half
    groups = c_ref.shape[0] // (levels * width)
    depth = jnp.where(sea_ref[...] > 0, wet_ref[...], 0).astype(F32)
    depth_ref[...] = depth
    for part, (west, east) in enumerate(((west_a, east_a), (west_b, east_b))):
        for i in range(width):
            side, n = (west, i) if i < HALO else (east, i - HALO)
            for t in range(groups + 2):
                ref, g = (c_ref, t) if t < groups else (face_ref, t - groups)
                first = (g * levels + part * half) * width + i
                side[n, pl.ds(t, half, stride=PAD), :] = ref[pl.ds(first, half, stride=width), :]
            side[n, groups + 2 : groups + 3, :] = depth[i : i + 1, :]


def factor_kernel(mix_ref, depth_ref, gone_ref, inverse_ref, ratio_ref):
    width = depth_ref.shape[0]
    levels = mix_ref.shape[0]
    depth = depth_ref[...]
    zero = jnp.zeros_like(depth)

    def step(k, carry):
        gone, ratio = carry
        reach = jnp.where(k < levels - 1, (k + 1).astype(F32), 1e9)
        down = jnp.where(depth > reach, mix_ref[k], 0.0)
        inverse = 1.0 / (1.0 + gone + down + gone * ratio)
        ratio = -down * inverse
        gone_ref[k] = gone
        inverse_ref[k] = inverse
        ratio_ref[k] = ratio
        return down, ratio

    lax.fori_loop(0, levels, step, (zero, zero), unroll=4)


def wide(row):
    return jnp.broadcast_to(row, (ROWS, LANES))


def cells_of(west_ref, east_ref, far_west_ref, far_east_ref, groups):
    columns = [(r, n) for r in (far_west_ref, west_ref, east_ref, far_east_ref) for n in range(HALO)]
    depth = [r[n, groups + 2 : groups + 3, :] for r, n in columns]
    return columns, depth


def sweep(columns, depth, groups, offset, gone_ref, inverse_ref, x_ref, stencil_ref, before):
    levels = columns[0][0].shape[1] // PAD
    cells = len(columns)
    width = cells - 2 * HALO
    parts = PAD // ROWS

    number = (iota((levels, LANES), 0) + offset).astype(F32)
    inner_north = iota((levels, LANES), 1) < LANES - 1
    active = [jnp.where(number < d, 1.0, 0.0) for d in depth]

    def face(f, e):
        r, n = columns[e]
        return r[n, pl.ds(groups + f, levels, stride=PAD), :]

    gain, loss = None, None
    for e in range(cells - 1):
        u = face(0, e) * (active[e] * active[e + 1])
        up, um = jnp.maximum(u, 0.0), jnp.minimum(u, 0.0)
        if e > 0:
            v = face(1, e) * active[e] * pltpu.roll(active[e], LANES - 1, 1)
            v = jnp.where(inner_north, v, 0.0)
            vp, vm = jnp.maximum(v, 0.0), jnp.minimum(v, 0.0)
            stencil_ref[e - 1, 0] = (1.0 - up + loss) + (pltpu.roll(vm, 1, 1) - vp)
            stencil_ref[e - 1, 1] = gain
            stencil_ref[e - 1, 2] = -um
            stencil_ref[e - 1, 3] = pltpu.roll(vp, 1, 1)
            stencil_ref[e - 1, 4] = -vm
        gain, loss = up, um

    def forward(k, before):
        after = []
        for h in range(parts):
            here = pl.ds(pl.multiple_of(k * PAD, PAD) + h * ROWS, ROWS)
            there = pl.ds(pl.multiple_of((k + offset) * PAD, PAD) + h * ROWS, ROWS)
            c = {e: r[n, here, :] for e, (r, n) in enumerate(columns)}
            for reach in (1, 2):
                new = {}
                for e in range(reach, cells - reach):
                    own, west, east, south, north = (
                        wide(stencil_ref[e - 1, f, pl.ds(k, 1), :]) for f in range(5)
                    )
                    new[e] = (
                        (own * c[e] + west * c[e - 1])
                        + east * c[e + 1]
                        + (south * pltpu.roll(c[e], 1, 1) + north * pltpu.roll(c[e], LANES - 1, 1))
                    )
                c = new
            for i in range(width):
                gone, inverse = (wide(r[k + offset, i : i + 1, :]) for r in (gone_ref, inverse_ref))
                p = (c[i + HALO] + gone * before[h * width + i]) * inverse
                x_ref[there, i * LANES : (i + 1) * LANES] = p
                after.append(p)
        return tuple(after)

    return lax.fori_loop(0, levels, forward, before, unroll=2)


def zero_rows(count):
    return tuple([jnp.zeros((ROWS, LANES), F32)] * count)


def upper_kernel(
    west_ref, east_ref, far_west_ref, far_east_ref, gone_ref, inverse_ref, x_ref, stencil_ref
):
    width = gone_ref.shape[1]
    groups = PAD - 4
    columns, depth = cells_of(west_ref, east_ref, far_west_ref, far_east_ref, groups)
    zeros = zero_rows(width * PAD // ROWS)
    sweep(columns, depth, groups, 0, gone_ref, inverse_ref, x_ref, stencil_ref, zeros)


def lower_kernel(
    west_ref,
    east_ref,
    far_west_ref,
    far_east_ref,
    gone_ref,
    inverse_ref,
    ratio_ref,
    side_ref,
    fold_ref,
    begun_ref,
    out_ref,
    x_ref,
    stencil_ref,
):
    levels = gone_ref.shape[0]
    width = gone_ref.shape[1]
    groups = out_ref.shape[1] * 2 // levels
    half = levels // 2
    parts = PAD // ROWS
    columns, depth = cells_of(west_ref, east_ref, far_west_ref, far_east_ref, groups)
    last = (half - 1) * PAD
    before = tuple(
        begun_ref[last + h * ROWS : last + (h + 1) * ROWS, i * LANES : (i + 1) * LANES]
        for h in range(parts)
        for i in range(width)
    )
    sweep(columns, depth, groups, half, gone_ref, inverse_ref, x_ref, stencil_ref, before)

    zeros = zero_rows(parts * width)

    def place(k, h, i):
        return pl.ds(pl.multiple_of(k * PAD, PAD) + h * ROWS, ROWS), pl.ds(i * LANES, LANES)

    def back_low(n, x):
        k = levels - 1 - n
        new = []
        for h in range(parts):
            for i in range(width):
                ratio = wide(ratio_ref[k, i : i + 1, :])
                value = x_ref[place(k, h, i)] - ratio * x[h * width + i]
                x_ref[place(k, h, i)] = value
                new.append(value)
        return tuple(new)

    side = side_ref[...]
    deep_depth, shallow_depth = [], []
    for i in range(width):
        kind = side[i : i + 1, :]
        deep_depth.append(wide(jnp.where(kind > 0.5, depth[i + HALO], 0.0)))
        shallow_depth.append(wide(jnp.where(kind < -0.5, depth[i + HALO], 0.0)))

    def back_high(n, x):
        k = half - 1 - n
        other = levels - 1 - k
        low, high = k.astype(F32), other.astype(F32)
        new = []
        for i in range(width):
            ratio = wide(ratio_ref[k, i : i + 1, :])
            deep_low, deep_high = deep_depth[i] > low, deep_depth[i] > high
            shallow_low, shallow_high = shallow_depth[i] > low, shallow_depth[i] > high
            for h in range(parts):
                value = begun_ref[place(k, h, i)] - ratio * x[i * parts + h]
                under = x_ref[place(other, h, i)]
                new.append(value)
                x_ref[place(k, h, i)] = jnp.where(deep_low, value, jnp.where(shallow_high, under, 0.0))
                x_ref[place(other, h, i)] = jnp.where(deep_high, under, jnp.where(shallow_low, value, 0.0))
        return tuple(new)

    x = lax.fori_loop(0, half, back_low, zeros, unroll=2)
    x = tuple(x[h * width + i] for i in range(width) for h in range(parts))
    lax.fori_loop(0, half, back_high, x, unroll=2)

    step = 4
    rows = step * PAD
    left = iota((step * groups, LANES), 1) < LANES // 2
    onehot = jnp.concatenate([fold_ref[i] for i in range(width)], axis=0)

    def send(n, _):
        k = n * step
        begin = pl.multiple_of(k * PAD, rows)
        both = jnp.concatenate(
            [x_ref[pl.ds(begin, rows), :], x_ref[pl.ds(begin + half * PAD, rows), :]], axis=0
        )
        whole = picked(both, onehot)
        whole = jnp.concatenate(
            [whole[j * PAD : j * PAD + groups] for j in range(2 * step)], axis=0
        )
        upper, lower = whole[: step * groups], whole[step * groups :]
        here = pl.ds(pl.multiple_of(k * groups, step * groups), step * groups)
        for v in range(upper.shape[1] // LANES):
            u = upper[:, v * LANES : (v + 1) * LANES]
            w = lower[:, v * LANES : (v + 1) * LANES]
            out_ref[2 * v, here, :] = jnp.where(left, u, pltpu.roll(w, LANES // 2, 1))
            out_ref[2 * v + 1, here, :] = jnp.where(left, pltpu.roll(u, LANES // 2, 1), w)
        return 0

    lax.fori_loop(0, half // step, send, 0)


def reaction_kernel(
    x_ref, lane_ref, matrix_ref, decay_ref, photic_ref, out_ref, state_ref, light_ref, chl_ref
):
    peers, rows, _ = x_ref.shape
    groups = matrix_ref.shape[0] // (2 * peers)
    half = rows // groups
    quarter = half // 2
    pad = light_ref.shape[0]
    chl_ref[...] = jnp.zeros_like(chl_ref)
    for k in range(half):
        chl_ref[k : k + 1, :] = x_ref[0, k * groups : k * groups + 1, :]
    attenuation = jnp.where(iota((pad, LANES), 0) < half, 0.05 + 0.1 * chl_ref[...], 0.0)
    before = jnp.where(iota((pad, pad), 1) < iota((pad, pad), 0), 1.0, 0.0).astype(F32)
    beyond = jnp.where(iota((pad, pad), 1) > iota((pad, pad), 0), 1.0, 0.0).astype(F32)
    above = jnp.dot(before, attenuation, precision=lax.Precision.HIGHEST, preferred_element_type=F32)
    under = jnp.dot(beyond, attenuation, precision=lax.Precision.HIGHEST, preferred_element_type=F32)
    total = jnp.broadcast_to(jnp.sum(attenuation, axis=0, keepdims=True), (pad, LANES))
    total = pltpu.roll(total, LANES // 2, 1)
    right = iota((pad, LANES), 1) >= LANES // 2
    above = above + jnp.where(right, total, 0.0)
    under = under + jnp.where(right, 0.0, total)
    level = (iota((pad, LANES), 0) + jnp.where(right, half, 0)).astype(F32)
    deep = level < lane_ref[0:1, :]
    light = jnp.exp(-jnp.where(deep, above, under))
    light_ref[...] = light
    heat = HEAT_GAIN * light * (1.0 - jnp.exp(-attenuation))
    chl_ref[...] = heat
    first, second = chl_ref[0:quarter, :], chl_ref[quarter : 2 * quarter, :]
    left = iota((quarter, LANES), 1) < LANES // 2
    outer, inner = jnp.where(left, first, second), jnp.where(left, second, first)
    for q in range(peers):
        out_ref[q, rows:, :] = jnp.zeros((out_ref.shape[1] - rows, LANES), F32)
        out_ref[q, rows : rows + quarter, :] = outer if q in (0, peers - 1) else inner

    span = 2 * groups
    decay = decay_ref[...]
    matrix = matrix_ref[...]
    hi = matrix.astype(BF16)
    low = (matrix - hi.astype(F32)).astype(BF16)
    both = jnp.concatenate([hi, hi], axis=1)
    photic_even, photic_odd = photic_ref[0], photic_ref[1]

    def run(pairs):
        state, push = [], []
        for m in pairs:
            state.append(
                jnp.concatenate([x_ref[s, m * span : (m + 1) * span, :] for s in range(peers)], axis=0)
            )
            push.append(
                photic_even * light_ref[2 * m : 2 * m + 1, :]
                + photic_odd * light_ref[2 * m + 1 : 2 * m + 2, :]
            )
        state, push = jnp.concatenate(state, axis=1), jnp.concatenate(push, axis=1)
        rate = jnp.concatenate([decay] * len(pairs), axis=1)
        for _ in range(SUBSTEPS):
            upper = state.astype(BF16)
            lower = (state - upper.astype(F32)).astype(BF16)
            forcing = (
                jnp.dot(both, jnp.concatenate([upper, lower], axis=0), preferred_element_type=F32)
                + jnp.dot(low, upper, preferred_element_type=F32)
                + push
            )
            state = state * rate + RATE_STEP * jnp.tanh(forcing)
        for n, m in enumerate(pairs):
            for s in range(peers):
                out_ref[s, m * span : (m + 1) * span, :] = state[
                    s * span : (s + 1) * span, n * LANES : (n + 1) * LANES
                ]

    for m in range(0, half // 2, 2):
        run((m, m + 1))


def return_kernel(
    x_ref, c_ref, thermal_ref, depth_ref, side_ref, unfold_ref, place_ref, out_ref, heat_ref, y_ref, h_ref
):
    groups, levels, width, _ = c_ref.shape
    share = thermal_ref.shape[0]
    half = levels // 2
    step = 4
    rows = step * groups
    left = iota((rows, LANES), 1) < LANES // 2
    unfold = unfold_ref[...]

    def spread(k, value):
        whole = picked(value, unfold)
        for i in range(width):
            first = pl.multiple_of(k * groups * ROWS, ROWS) + i
            y_ref[pl.ds(first, rows, stride=ROWS), :] = whole[:, i * LANES : (i + 1) * LANES]

    def open_up(n, _):
        k = n * step
        here = pl.ds(pl.multiple_of(k * groups, rows), rows)
        upper, lower = [], []
        for v in range(x_ref.shape[0] // 2):
            p, q = x_ref[2 * v, here, :], x_ref[2 * v + 1, here, :]
            upper.append(jnp.where(left, p, pltpu.roll(q, LANES // 2, 1)))
            lower.append(jnp.where(left, pltpu.roll(p, LANES // 2, 1), q))
        spread(k, jnp.concatenate(upper, axis=1))
        spread(k + half, jnp.concatenate(lower, axis=1))
        return 0

    lax.fori_loop(0, half // step, open_up, 0)

    depth = depth_ref[...]
    side = side_ref[...]
    deep_depth = jnp.where(side > 0.5, depth, 0.0)
    shallow_depth = jnp.where(side < -0.5, depth, 0.0)

    def merge(k, _):
        other = levels - 1 - k
        deep = deep_depth > k.astype(F32)
        shallow = shallow_depth > k.astype(F32)
        for t in range(groups):
            one = y_ref[pl.ds(pl.multiple_of((k * groups + t) * ROWS, ROWS), width), :]
            two = y_ref[pl.ds(pl.multiple_of((other * groups + t) * ROWS, ROWS), width), :]
            out_ref[t, k] = jnp.where(deep, one, jnp.where(shallow, two, c_ref[t, k]))
        return 0

    lax.fori_loop(0, levels, merge, 0)

    place = place_ref[0]
    begin = groups * half
    halves = ([], [])
    left = iota((share, LANES), 1) < LANES // 2
    for v in range(x_ref.shape[0] // 2):
        p, q = (x_ref[2 * v + n, begin : begin + share, :] for n in (0, 1))
        halves[0].append(jnp.where(left, p, pltpu.roll(q, LANES // 2, 1)))
        halves[1].append(jnp.where(left, pltpu.roll(p, LANES // 2, 1), q))
    first, second = (jnp.concatenate(h, axis=1) for h in halves)
    upper_half = place < 2
    deep_heat = jnp.where(upper_half, first, second)
    shallow_heat = jnp.where(upper_half, second, first)
    flip = jnp.where(iota((share, share), 0) + iota((share, share), 1) == share - 1, 1.0, 0.0)
    shallow_heat = jnp.dot(
        flip.astype(F32), shallow_heat, precision=lax.Precision.HIGHEST, preferred_element_type=F32
    )
    for n, part in enumerate((deep_heat, shallow_heat)):
        whole = picked(part, unfold)
        for i in range(width):
            h_ref[n, pl.ds(i, share, stride=ROWS), :] = whole[:, i * LANES : (i + 1) * LANES]
    for k in range(share):
        level = (place * share + k).astype(F32)
        one, two = h_ref[0, k * ROWS : k * ROWS + width, :], h_ref[1, k * ROWS : k * ROWS + width, :]
        warm = jnp.where(deep_depth > level, one, jnp.where(shallow_depth > level, two, 0.0))
        heat_ref[k] = thermal_ref[k] + warm


def ring(axis):
    count = lax.axis_size(axis)
    forward = [(i, i + 1) for i in range(count - 1)]
    return forward, [(b, a) for a, b in forward]


def body(
    species_concentration,
    courant_face_numbers,
    diffusive_interface_factor,
    thermal_anomaly_field,
    seawater_indicator,
    wet_layer_number,
    species_coupling_matrix,
    species_photic_factor,
    species_loss_factor,
):
    groups, levels, width, _ = species_concentration.shape
    share = diffusive_interface_factor.shape[0]
    peers = lax.axis_size("comp")
    half = levels // 2
    columns = width * LANES
    lanes = columns // 2
    place = lax.axis_index("comp")
    sds = jax.ShapeDtypeStruct

    slices = jnp.concatenate([courant_face_numbers, diffusive_interface_factor[None]], axis=0)
    faces = lax.all_gather(slices, "comp", axis=1, tiled=True)
    strip = sds((HALO, half * PAD, LANES), F32)
    west_a, west_b, east_a, east_b, depth = call(
        split_kernel, (strip, strip, strip, strip, sds((width, LANES), F32)), ins=[VMEM] * 4
    )(
        species_concentration.reshape(groups * levels * width, LANES),
        faces.reshape(-1, LANES),
        seawater_indicator,
        wet_layer_number,
    )
    onward, backward = ring("tile")
    far_west_a = lax.ppermute(east_a, "tile", onward)
    far_east_a = lax.ppermute(west_a, "tile", backward)
    far_west_b = lax.ppermute(east_b, "tile", onward)
    far_east_b = lax.ppermute(west_b, "tile", backward)
    gone, inverse, ratio = call(
        factor_kernel,
        tuple(sds((levels, width, LANES), F32) for _ in range(3)),
        ins=[VMEM] * 2,
    )(faces[2], depth)

    fold, unfold, rank, lane_depth = call(
        lambda *refs: pairing_kernel(levels, *refs),
        (
            sds((width, LANES, lanes), BF16),
            sds((lanes, columns), BF16),
            sds((ROWS, LANES), F32),
            sds((ROWS, lanes), F32),
        ),
        ins=[VMEM],
    )(depth)
    rank = rank[:width]
    over = lane_depth[2, 0] > 0.5
    deep = rank < float(lanes)
    eye = jnp.eye(2, dtype=F32)
    matrix = species_coupling_matrix.reshape(peers, groups, peers, groups)
    matrix = matrix[:, None, :, :, None, :] * eye[None, :, None, None, :, None]
    matrix = matrix.reshape(peers * 2 * groups, peers * 2 * groups)

    def spreadable(vector):
        v = jnp.broadcast_to(vector.reshape(peers, 1, groups, 1), (peers, 2, groups, LANES))
        return v

    decay = spreadable(1.0 - RATE_STEP * species_loss_factor).reshape(-1, LANES)
    photic = spreadable(species_photic_factor)[None] * eye[:, None, :, None, None]
    photic = photic.reshape(2, -1, LANES)

    stencil = pltpu.VMEM((width + 2, 5, half, LANES), F32)
    begun = call(
        upper_kernel, sds((half * PAD, columns), F32), scratch=[stencil], ins=[VMEM] * 6
    )(west_a, east_a, far_west_a, far_east_a, gone, inverse)

    def round_trip(current, temperature, side, a, b):
        folded = call(
            lower_kernel,
            sds((peers, half * groups, LANES), F32),
            scratch=[pltpu.VMEM((levels * PAD, columns), F32), stencil],
            ins=[VMEM] * 10,
        )(west_b, east_b, far_west_b, far_east_b, gone, inverse, ratio, side, fold, begun)
        arrived = lax.all_to_all(folded, "comp", split_axis=0, concat_axis=0, tiled=True)
        part = lanes // peers
        mine = lax.dynamic_slice_in_dim(jnp.stack([a, b]), place * part, part, axis=1)
        mine = jnp.pad(jnp.concatenate([mine, mine], axis=1), ((0, ROWS - 2), (0, 0)))
        extra = -(-share // ROWS) * ROWS
        reacted = call(
            reaction_kernel,
            sds((peers, half * groups + extra, LANES), F32),
            scratch=[
                pltpu.VMEM((ROWS, LANES), F32),
                pltpu.VMEM((-(-half // ROWS) * ROWS, LANES), F32),
                pltpu.VMEM((-(-half // ROWS) * ROWS, LANES), F32),
            ],
            ins=[VMEM] * 5,
        )(arrived, mine, matrix, decay, photic)
        returned = lax.all_to_all(reacted, "comp", split_axis=0, concat_axis=0, tiled=True)
        return call(
            return_kernel,
            (
                sds((groups, levels, width, LANES), F32),
                sds((share, width, LANES), F32),
            ),
            scratch=[
                pltpu.VMEM((levels * groups * ROWS, LANES), F32),
                pltpu.VMEM((2, -(-share // ROWS) * ROWS * ROWS, LANES), F32),
            ],
            ins=[VMEM] * 6 + [SMEM],
        )(returned, current, temperature, depth, side, unfold, place[None].astype(jnp.int32))

    a, b = lane_depth[0], lane_depth[1]
    sign = jnp.where(deep, 1.0, -1.0).astype(F32)
    side = jnp.where(over & ~deep, 0.0, sign)
    out, heat = round_trip(
        species_concentration, thermal_anomaly_field, side, a, jnp.where(over, 0.0, b)
    )

    def rest(carry):
        _, current, temperature = carry
        current, temperature = round_trip(
            current, temperature, jnp.where(deep, 0.0, sign), jnp.zeros_like(a), b
        )
        return jnp.zeros((), bool), current, temperature

    _, out, heat = lax.while_loop(lambda carry: carry[0], rest, (over, out, heat))
    return out, heat


def solution(mesh):
    in_specs = (
        P("comp", None, "tile", None),
        P(None, "comp", "tile", None),
        P("comp", "tile", None),
        P("comp", "tile", None),
        P("tile", None),
        P("tile", None),
        P(),
        P(),
        P(),
    )
    out_specs = (P("comp", None, "tile", None), P("comp", "tile", None))
    return jax.shard_map(body, mesh=mesh, in_specs=in_specs, out_specs=out_specs, check_vma=False)
```
